128 devices in a mesh: sub: 8 (over z, core), grp: 16 (over x, y).
Axes of the slice: x: 4, y: 4, z: 4, core: 2. Of those that a mesh axis runs over, the one named last changes fastest.
Arguments:
- schur: bfloat16 [512, 1024, 1024], P(('sub', 'grp')), as said below
- mortar: bfloat16 [512, 8, 128, 128], P(('sub', 'grp')), may hold values from -0.5 to 0.5
- partner: int32 [512, 4], P(('sub', 'grp')), may hold values from 0 to 15, as said below
- corner_map: int32 [512, 8], P(('sub', 'grp')), may hold values from 0 to 127
- coarse_inv: float32 [8, 128, 128], P('sub'), as said below
- load: float32 [512, 1024, 384], P(('sub', 'grp')), may hold values from -6 to 6
Outputs:
- solution: float32 [512, 1024, 384], P(('sub', 'grp'))
The draws below stay inside these ranges and needn't reach their ends.
Inputs may be any that keep to these rules, and one draw needn't show every extreme that they name: `partner`: within the 4 subdomains of one device, the entries form a permutation of 0 to 15. `schur`: each matrix is symmetric positive definite. `coarse_inv`: each matrix is symmetric positive definite.
All inputs are finite; a program needn't handle non-finite values.
Results may differ from the reference program's by a relative error of at most 0.0025.
Values may be sent and summed in bfloat16 or wider, within the bound.
A program may use at most 128 MiB of HBM per device.

```python
import math
import jax
import jax.numpy as jnp
from jax import lax

IF = 1024
FB = 128
NF = 8
NCR = 8
NCO = 128
SUBDEV = 4
RHS = 384
ITERS = 2
SUBS = 512
N_SUB = 8
N_GRP = 16


def symmetric_block(key, order, spread, low, high):
    first_key, second_key = jax.random.split(key)
    noise = jax.random.normal(first_key, (order, order), jnp.float32)
    scaled = (noise + noise.T) * (spread / math.sqrt(2.0 * order))
    diagonal = jnp.exp(jax.random.uniform(second_key, (order, 1), jnp.float32, math.log(low), math.log(high)))
    identity = (lax.broadcasted_iota(jnp.int32, (order, order), 0) == lax.broadcasted_iota(jnp.int32, (order, order), 1)).astype(jnp.float32)
    return scaled + identity * diagonal


def draw_schur(key, part):

    def single(index):
        return symmetric_block(jax.random.fold_in(key, index), IF, 0.9, 2.5, 6.0).astype(jnp.bfloat16)
    return lax.map(single, jnp.arange(SUBS, dtype=jnp.int32))


def draw_coarse_inv(key, part):

    def single(index):
        return symmetric_block(jax.random.fold_in(key, index + 7), NCO, 0.4, 1.2, 3.0)
    return lax.map(single, jnp.arange(N_SUB, dtype=jnp.int32))


def draw_partner(key, part):
    device_keys = jax.random.split(jax.random.fold_in(key, 11), SUBS // SUBDEV)
    orders = jax.vmap(lambda single: jax.random.permutation(single, SUBDEV * (NF // 2)))(device_keys)
    return orders.astype(jnp.int32).reshape(SUBS, NF // 2)


def draw_corner_map(key, part):
    mapping = jax.random.randint(jax.random.fold_in(key, 13), (SUBS, NCR), 0, NCO, jnp.int32)
    return mapping.at[0, 0].set(NCO - 1).at[0, 1].set(0)


def block_scale(stream_key, dims, pieces, least, largest):
    level, own = 1.0, jax.random.fold_in(stream_key, 6)
    for position, blocks in pieces:
        draws = jnp.exp(jax.random.uniform(jax.random.fold_in(own, position), (blocks,), jnp.float32, least / len(pieces), largest / len(pieces)))
        level = level * jnp.repeat(draws, dims[position] // blocks).reshape([-1 if axis == position else 1 for axis in range(len(dims))])
    return level


def normal_values(rng, dims, scale, limit, shards=(), held_as=jnp.bfloat16):
    level = block_scale(rng, dims, shards, -0.22, 0.18) if shards else 1.0
    values = jax.random.normal(rng, dims, jnp.float32) * scale * level
    return jnp.minimum(jnp.maximum(values, -limit), limit).astype(held_as)


def setup_inputs(seed: int = 0) -> dict:
    seeds = jax.random.split(jax.random.key(seed), 7)
    schur = draw_schur(jax.random.fold_in(seeds[6], 71), 0)
    mortar = normal_values(seeds[1], (SUBS, NF, FB, FB), FB ** -0.5, 0.5, ((0, 128),))
    partner = draw_partner(jax.random.fold_in(seeds[6], 71), 0)
    corner_map = draw_corner_map(jax.random.fold_in(seeds[6], 71), 0)
    coarse_inv = draw_coarse_inv(jax.random.fold_in(seeds[6], 71), 0)
    load = normal_values(seeds[5], (SUBS, IF, RHS), 1.0, 6.0, ((0, 128),), jnp.float32)
    return dict(schur=schur, mortar=mortar, partner=partner, corner_map=corner_map, coarse_inv=coarse_inv, load=load)


def operate(direction, schur, mortar, mates, inverse, grouped_hot, coarse_inv):
    half_faces = NF // 2
    stride = IF // NCR
    dir_half = direction.astype(jnp.bfloat16)
    stiff = lax.map(lambda couple: jnp.dot(couple[0], couple[1], preferred_element_type=jnp.float32), (schur, dir_half))
    face_rows = dir_half.reshape(SUBS, NF, FB, RHS)
    traces = lax.map(lambda couple: jnp.einsum("fij,fjr->fir", couple[0].astype(jnp.float32), couple[1].astype(jnp.float32)), (mortar, face_rows)).astype(jnp.bfloat16)
    shaped = traces.reshape(N_SUB, N_GRP, SUBDEV, NF, FB, RHS)
    upper = shaped[:, :, :, :half_faces].reshape(N_SUB, N_GRP, SUBDEV * half_faces, FB, RHS)
    lower = shaped[:, :, :, half_faces:].reshape(N_SUB, N_GRP, SUBDEV * half_faces, FB, RHS)
    above = jnp.roll(lower, -1, axis=0)
    upper_mate = jnp.take_along_axis(above, mates[:, :, :, None, None], axis=2)
    reordered = jnp.take_along_axis(upper, inverse[:, :, :, None, None], axis=2)
    lower_mate = jnp.roll(reordered, 1, axis=0)
    jump_upper = (upper.astype(jnp.float32) - upper_mate.astype(jnp.float32)).astype(jnp.bfloat16)
    jump_lower = (lower.astype(jnp.float32) - lower_mate.astype(jnp.float32)).astype(jnp.bfloat16)
    jump_all = jnp.concatenate([jump_upper.reshape(N_SUB, N_GRP, SUBDEV, half_faces, FB, RHS), jump_lower.reshape(N_SUB, N_GRP, SUBDEV, half_faces, FB, RHS)], axis=3).reshape(SUBS, NF, FB, RHS)
    pulled = lax.map(lambda couple: jnp.einsum("fji,fjr->fir", couple[0].astype(jnp.float32), couple[1].astype(jnp.float32)), (mortar, jump_all))
    partial_value = stiff + pulled.reshape(SUBS, IF, RHS)
    corners = direction[:, ::stride, :].reshape(N_SUB, N_GRP * SUBDEV, NCR, RHS)
    coarse_sum = jnp.einsum("nsco,nscr->nor", grouped_hot, corners, precision=lax.Precision.HIGHEST)
    coarse_val = jnp.einsum("nop,npr->nor", coarse_inv, coarse_sum, precision=lax.Precision.HIGHEST)
    corner_add = jnp.einsum("nsco,nor->nscr", grouped_hot, coarse_val, precision=lax.Precision.HIGHEST).reshape(SUBS, NCR, RHS)
    return partial_value.at[:, ::stride, :].add(corner_add)


def reference(schur, mortar, partner, corner_map, coarse_inv, load):
    half_faces = NF // 2
    mates = partner.reshape(N_SUB, N_GRP, SUBDEV * half_faces).astype(jnp.int32)
    inverse = jnp.argsort(mates, axis=-1).astype(jnp.int32)
    onehot = (corner_map[..., None] == jnp.arange(NCO, dtype=jnp.int32)).astype(jnp.float32)
    grouped_hot = onehot.reshape(N_SUB, N_GRP * SUBDEV, NCR, NCO)
    solution = jnp.zeros_like(load)
    residual = load
    direction = load
    norm_now = jnp.sum(residual * residual, axis=(0, 1))
    for step in range(ITERS):
        image = operate(direction, schur, mortar, mates, inverse, grouped_hot, coarse_inv)
        step_len = norm_now / jnp.sum(direction * image, axis=(0, 1))
        solution = solution + step_len * direction
        if step + 1 < ITERS:
            residual = residual - step_len * image
            norm_next = jnp.sum(residual * residual, axis=(0, 1))
            direction = residual + (norm_next / norm_now) * direction
            norm_now = norm_next
    return solution
```

```python
import functools

import jax
import jax.numpy as jnp
from jax import lax
from jax.experimental import pallas as pl
from jax.experimental.pallas import tpu as pltpu
from jax.sharding import PartitionSpec as P

F32, BF16 = jnp.float32, jnp.bfloat16
SUBDOMS, HALF, FACES = 4, 4, 8
BLOCK, COLS, ORDER = 128, 384, 1024
ALL, SLOTS, COARSE = 32, 16, 128
SIDE = 4
N_SUB = 8
N_GRP = 16
UP = 7
MESH = pl.DeviceIdType.MESH
EXACT = lax.Precision.HIGHEST


def low(s, k):
    return s * FACES + HALF + k


def rows8(a):
    return jnp.sum(a.reshape(BLOCK // 8, 8, COLS), axis=0)


def one_row(acc):
    return jnp.sum(acc, axis=0, keepdims=True)


def mul(a, b):
    return jnp.dot(a, b, preferred_element_type=F32)


def mul_t(a, b):
    return lax.dot_general(a, b, (((0,), (0,)), ((), ())), preferred_element_type=F32)


def kernel(
    schur_h, mortar_h, load_h, coarse_h, partner, cmap, out_h,
    S, M, B, K, VB, Q, RB, TR, SU, AB, MT, JU, TQ, SU2, RU2, RD2,
    OH, CR, CX, RX, CY, RY, GY, GX, CA, RS, AS, AX, AY, AZ, INV,
    load_s, mort_s, schur_s, coarse_s, out_s,
    sd_s, sd_r, su_s, su_r, td_s, td_r, tu_s, tu_r,
    g_s, g_r, z_s, z_r, f_s, f_r,
):
    sub, grp = lax.axis_index("sub"), lax.axis_index("grp")
    gx, gy = grp // SIDE, grp % SIDE
    above, below = (sub + 1) % N_SUB, (sub + N_SUB - 1) % N_SUB

    def along_x(d):
        return {"grp": ((gx + d) % SIDE) * SIDE + gy}

    def along_y(d):
        return {"grp": gx * SIDE + (gy + d) % SIDE}

    def along_sub(d):
        return {"sub": (sub + d) % N_SUB}

    def send(src, dst, ssem, rsem, device):
        return pltpu.make_async_remote_copy(
            src_ref=src, dst_ref=dst, send_sem=ssem, recv_sem=rsem,
            device_id=device, device_id_type=MESH,
        )

    def send_down(j):
        s, k = j // HALF, j % HALF
        return send(TR.at[low(s, k)], AB.at[j], sd_s.at[j], sd_r.at[j], {"sub": below})

    def send_up(j):
        return send(SU.at[j], MT.at[j], su_s.at[j], su_r.at[j], {"sub": above})

    def send_up2(j):
        return send(SU2.at[j], RU2.at[j], tu_s.at[j], tu_r.at[j], {"sub": above})

    def send_down2(j):
        s, k = j // HALF, j % HALF
        return send(
            TQ.at[low(s, k)], RD2.at[j - UP], td_s.at[j - UP], td_r.at[j - UP], {"sub": below}
        )

    mort_c = pltpu.make_async_copy(mortar_h, M, mort_s)
    mort_c.start()

    def load_c(s):
        span = pl.ds(s * FACES, FACES)
        return pltpu.make_async_copy(load_h.at[span], B.at[span], load_s.at[s])

    def schur_c(s):
        return pltpu.make_async_copy(schur_h.at[s], S.at[s], schur_s.at[s])

    coarse_c = pltpu.make_async_copy(coarse_h.at[0], K, coarse_s)
    for s in range(SUBDOMS):
        load_c(s).start()
    coarse_c.start()
    for s in range(SUBDOMS):
        schur_c(s).start()

    barrier = pltpu.get_barrier_semaphore()
    for d in range(1, SIDE):
        pl.semaphore_signal(barrier, inc=1, device_id=along_x(d), device_id_type=MESH)
        pl.semaphore_signal(barrier, inc=1, device_id=along_y(d), device_id_type=MESH)
    for d in range(1, N_SUB):
        pl.semaphore_signal(barrier, inc=1, device_id=along_sub(d), device_id_type=MESH)

    @pl.loop(0, SLOTS)
    def _(j):
        found = jnp.int32(0)
        for u in range(SLOTS):
            at = (u // HALF) * FACES + u % HALF
            found = jnp.where(partner[u // HALF, u % HALF] == j, at, found)
        INV[j] = found

    lanes = lax.broadcasted_iota(jnp.int32, (1, COARSE), 1)

    @pl.loop(0, SUBDOMS)
    def _(s):
        for c in range(FACES):
            OH[pl.ds(s * FACES + c, 1), :] = jnp.where(lanes == cmap[s, c], 1.0, 0.0).astype(F32)

    mort_c.wait()

    def first(s, acc):
        load_c(s).wait()
        for f in range(FACES):
            g = s * FACES + f
            b = B[g]
            acc = acc + rows8(b * b)
            half = b.astype(BF16)
            VB[g] = half
            TR[g] = mul(M[g], half).astype(BF16)
        return acc

    acc0 = lax.fori_loop(0, SUBDOMS, first, jnp.zeros((8, COLS), F32))
    pl.semaphore_wait(barrier, 2 * (SIDE - 1) + N_SUB - 1)

    @pl.loop(0, SLOTS)
    def _(j):
        send_down(j).start()
        SU[j] = TR[INV[j]]
        send_up(j).start()

    def coarse_pass(p, fields, row0, row1, work):
        @pl.loop(0, ALL)
        def _(g):
            CR[pl.ds(g, 1), :] = fields[g, 0:1, :]

        local = lax.dot_general(
            OH[...], CR[...], (((0,), (0,)), ((), ())), precision=EXACT, preferred_element_type=F32
        )
        for i in range(SIDE):
            CX[p, i, 0:32, :] = local[32 * i : 32 * i + 32]
            CX[p, i, 32:33, :] = row0
            CX[p, i, 33:34, :] = row1
            CX[p, i, 34:40, :] = jnp.zeros((6, COLS), F32)

        def rs_x(d):
            return send(
                CX.at[p, (gx + d) % SIDE], RX.at[p, d - 1], g_s.at[p, 0, d - 1], g_r.at[p, 0, d - 1],
                along_x(d),
            )

        def rs_y(d):
            return send(
                CY.at[p, (gy + d) % SIDE], RY.at[p, d - 1], g_s.at[p, 1, d - 1], g_r.at[p, 1, d - 1],
                along_y(d),
            )

        def ag_y(d):
            return send(
                GY.at[p, gy], GY.at[p, gy], g_s.at[p, 2, d - 1], g_r.at[p, 2, d - 1], along_y(d)
            )

        def ag_x(d):
            return send(
                GX.at[p, gx], GX.at[p, gx], g_s.at[p, 3, d - 1], g_r.at[p, 3, d - 1], along_x(d)
            )

        dist = range(1, SIDE)
        for d in dist:
            rs_x(d).start()
        work(0)
        for d in dist:
            rs_x(d).wait_recv()
        total = CX[p, gx] + RX[p, 0] + RX[p, 1] + RX[p, 2]
        for i in range(SIDE):
            CY[p, i, 0:8, :] = total[8 * i : 8 * i + 8]
            CY[p, i, 8:16, :] = total[32:40]
        for d in dist:
            rs_y(d).start()
        work(1)
        for d in dist:
            rs_y(d).wait_recv()
        total = CY[p, gy] + RY[p, 0] + RY[p, 1] + RY[p, 2]
        GY[p, gy] = total[0:8]
        for d in dist:
            ag_y(d).start()
        work(2, total[8:16])
        for d in dist:
            ag_y(d).wait_recv()
        GX[p, gx] = GY[p].reshape(32, COLS)
        for d in dist:
            ag_x(d).start()
        work(3)
        for d in dist:
            ag_x(d).wait_recv()
        for d in dist:
            rs_x(d).wait_send()
            rs_y(d).wait_send()
            ag_y(d).wait_send()
            ag_x(d).wait_send()
        return GX[p].reshape(COARSE, COLS)

    TILE = 512

    def stiff(s, *_):
        schur_c(s).wait()
        field = VB[s * FACES : (s + 1) * FACES].reshape(ORDER, COLS)

        @pl.loop(0, ORDER // TILE)
        def _(i):
            part = mul(S[s, pl.ds(pl.multiple_of(i * TILE, TILE), TILE), :], field)
            Q[pl.ds(s * FACES + i * (TILE // BLOCK), TILE // BLOCK)] = part.reshape(
                TILE // BLOCK, BLOCK, COLS
            )

    zero = jnp.zeros((1, COLS), F32)
    coarse_c.wait()
    sum_b = coarse_pass(0, B, zero, zero, stiff)
    coarse_val = jnp.dot(K[...], sum_b, precision=EXACT, preferred_element_type=F32)
    CA[...] = jnp.dot(OH[...], coarse_val, precision=EXACT, preferred_element_type=F32)

    def finish(g, mate, acc):
        jump = (TR[g].astype(F32) - mate.astype(F32)).astype(BF16)
        JU[g] = jump
        Q[g] = Q[g] + mul_t(M[g], jump)
        Q[g, 0:1, :] = Q[g, 0:1, :] + CA[pl.ds(g, 1), :]
        q = Q[g]
        TQ[g] = mul(M[g], q.astype(BF16)).astype(BF16)
        return acc + rows8(B[g] * q)

    @pl.loop(0, SLOTS)
    def _(j):
        send_down(j).wait_recv()

    def upper(s, acc):
        for k in range(HALF):
            acc = finish(s * FACES + k, AB[partner[s, k]], acc)
        return acc

    acc1 = lax.fori_loop(0, SUBDOMS, upper, jnp.zeros((8, COLS), F32))

    @pl.loop(0, UP)
    def _(j):
        SU2[j] = TQ[INV[j]]
        send_up2(j).start()

    def lower(s, acc):
        for k in range(HALF):
            send_up(s * HALF + k).wait_recv()
            acc = finish(low(s, k), MT[s * HALF + k], acc)
        return acc

    acc1 = lax.fori_loop(0, SUBDOMS, lower, acc1)

    @pl.loop(UP, SLOTS)
    def _(j):
        send_down2(j).start()

    others = range(1, N_SUB)

    def over_sub(d):
        return send(RS.at[0], RS.at[d], z_s.at[d - 1], z_r.at[d - 1], along_sub(d))

    def work2(i, scalars=None):
        if i == 2:
            RS[0] = scalars
            for d in others:
                over_sub(d).start()

    sum_q = coarse_pass(1, Q, one_row(acc0), one_row(acc1), work2)
    for d in others:
        over_sub(d).wait_recv()
    sums = RS[0]
    for d in others:
        sums = sums + RS[d]
    norm0, curve0 = sums[0:1], sums[1:2]
    step0 = norm0 / curve0

    def resid(s, carry):
        n1, gq = carry
        for f in range(FACES):
            g = s * FACES + f
            q = Q[g]
            r = B[g] - step0 * q
            n1 = n1 + rows8(r * r)
            gq = gq + rows8(r * q)
            Q[g] = r
            RB[g] = r.astype(BF16)
        return n1, gq

    acc_n, acc_g = lax.fori_loop(
        0, SUBDOMS, resid, (jnp.zeros((8, COLS), F32), jnp.zeros((8, COLS), F32))
    )

    energy = jnp.zeros((8, COLS), F32)
    for s in range(SUBDOMS):
        field = RB[s * FACES : (s + 1) * FACES].reshape(ORDER, COLS)

        def tile(i, acc, s=s, field=field):
            part = mul(S[s, pl.ds(pl.multiple_of(i * TILE, TILE), TILE), :], field)
            for t in range(TILE // BLOCK):
                r = Q[s * FACES + i * (TILE // BLOCK) + t]
                acc = acc + rows8(r * part[t * BLOCK : (t + 1) * BLOCK])
            return acc

        energy = lax.fori_loop(0, ORDER // TILE, tile, energy)

    sum_r = sum_b - step0 * sum_q
    coarse_r = jnp.dot(K[...], sum_r, precision=EXACT, preferred_element_type=F32)
    energy = energy + rows8(sum_r * coarse_r) * (1.0 / N_GRP)

    def pair(first_jump, own, other, acc):
        second = own.astype(F32) - other.astype(F32)
        r = first_jump.astype(F32) - step0 * second
        return acc + rows8(r * r)

    def pair_low(j, acc):
        send_up2(j).wait_recv()
        g = low(j // HALF, j % HALF)
        return pair(JU[g], TQ[g], RU2[j], acc)

    energy = lax.fori_loop(0, UP, pair_low, energy)

    def pair_up(j, acc):
        send_down2(j).wait_recv()
        g = INV[j]
        return pair(JU[g], TQ[g], RD2[j - UP], acc)

    energy = lax.fori_loop(UP, SLOTS, pair_up, energy)

    AS[0, 0:1, :] = one_row(acc_n)
    AS[0, 1:2, :] = one_row(acc_g)
    AS[0, 2:3, :] = one_row(energy)
    AS[0, 3:8, :] = jnp.zeros((5, COLS), F32)

    def stage(i, buf, n, where):
        def copy(d):
            return send(AS.at[i], buf.at[d - 1], f_s.at[i, d - 1], f_r.at[i, d - 1], where(d))

        for d in range(1, n):
            copy(d).start()
        for d in range(1, n):
            copy(d).wait_recv()
        total = AS[i]
        for d in range(1, n):
            total = total + buf[d - 1]
        for d in range(1, n):
            copy(d).wait_send()
        return total

    AS[1] = stage(0, AX, SIDE, along_x)
    AS[2] = stage(1, AY, SIDE, along_y)
    sums = stage(2, AZ, N_SUB, along_sub)
    norm1, cross, energy1 = sums[0:1], sums[1:2], sums[2:3]
    beta = norm1 / norm0
    curve1 = energy1 + 2.0 * beta * cross + beta * beta * curve0
    step1 = norm1 / curve1
    with_load = step0 + step1 * beta

    def out_c(s):
        span = pl.ds(s * FACES, FACES)
        return pltpu.make_async_copy(Q.at[span], out_h.at[span], out_s.at[s])

    @pl.loop(0, SUBDOMS)
    def _(s):
        for f in range(FACES):
            g = s * FACES + f
            Q[g] = with_load * B[g] + step1 * Q[g]
        out_c(s).start()

    @pl.loop(0, SLOTS)
    def _(j):
        send_down(j).wait_send()
        send_up(j).wait_send()

    @pl.loop(0, UP)
    def _(j):
        send_up2(j).wait_send()

    @pl.loop(UP, SLOTS)
    def _(j):
        send_down2(j).wait_send()

    for d in others:
        over_sub(d).wait_send()
    for s in range(SUBDOMS):
        out_c(s).wait()


def on_device(schur, mortar, partner, corner_map, coarse_inv, load):
    vm, dma = pltpu.VMEM, pltpu.SemaphoreType.DMA
    anywhere = pl.BlockSpec(memory_space=pl.ANY)
    scalar = pl.BlockSpec(memory_space=pltpu.SMEM)
    faces_half = (ALL, BLOCK, COLS)
    slots_half = (SLOTS, BLOCK, COLS)
    scratch = [
        vm((SUBDOMS, ORDER, ORDER), BF16),
        vm((ALL, BLOCK, BLOCK), BF16),
        vm(faces_half, F32),
        vm((COARSE, COARSE), F32),
        vm(faces_half, BF16),
        vm(faces_half, F32),
        vm(faces_half, BF16),
        vm(faces_half, BF16),
        vm(slots_half, BF16),
        vm(slots_half, BF16),
        vm(slots_half, BF16),
        vm(faces_half, BF16),
        vm(faces_half, BF16),
        vm((UP, BLOCK, COLS), BF16),
        vm((UP, BLOCK, COLS), BF16),
        vm((SLOTS - UP, BLOCK, COLS), BF16),
        vm((ALL, COARSE), F32),
        vm((ALL, COLS), F32),
        vm((2, SIDE, 40, COLS), F32),
        vm((2, SIDE - 1, 40, COLS), F32),
        vm((2, SIDE, 16, COLS), F32),
        vm((2, SIDE - 1, 16, COLS), F32),
        vm((2, SIDE, 8, COLS), F32),
        vm((2, SIDE, 32, COLS), F32),
        vm((ALL, COLS), F32),
        vm((N_SUB, 8, COLS), F32),
        vm((3, 8, COLS), F32),
        vm((SIDE - 1, 8, COLS), F32),
        vm((SIDE - 1, 8, COLS), F32),
        vm((N_SUB - 1, 8, COLS), F32),
        pltpu.SMEM((SLOTS,), jnp.int32),
        dma((SUBDOMS,)), dma, dma((SUBDOMS,)), dma, dma((SUBDOMS,)),
        dma((SLOTS,)), dma((SLOTS,)), dma((SLOTS,)), dma((SLOTS,)),
        dma((SLOTS - UP,)), dma((SLOTS - UP,)), dma((UP,)), dma((UP,)),
        dma((2, 4, SIDE - 1)), dma((2, 4, SIDE - 1)),
        dma((N_SUB - 1,)), dma((N_SUB - 1,)),
        dma((3, N_SUB - 1)), dma((3, N_SUB - 1)),
    ]
    out = pl.pallas_call(
        kernel,
        out_shape=jax.ShapeDtypeStruct((ALL, BLOCK, COLS), F32),
        in_specs=[anywhere] * 4 + [scalar] * 2,
        out_specs=anywhere,
        scratch_shapes=scratch,
        compiler_params=pltpu.CompilerParams(
            collective_id=0, has_side_effects=True, vmem_limit_bytes=60 * 1024 * 1024
        ),
    )(
        schur,
        mortar.reshape(ALL, BLOCK, BLOCK),
        load.reshape(ALL, BLOCK, COLS),
        coarse_inv,
        partner,
        corner_map,
    )
    return out.reshape(SUBDOMS, ORDER, COLS)


def solution(mesh):
    return jax.shard_map(
        on_device,
        mesh=mesh,
        in_specs=(
            P(("sub", "grp"), None, None),
            P(("sub", "grp"), None, None, None),
            P(("sub", "grp"), None),
            P(("sub", "grp"), None),
            P("sub", None, None),
            P(("sub", "grp"), None, None),
        ),
        out_specs=P(("sub", "grp"), None, None),
        check_vma=False,
    )
```

```python
import functools

import jax
import jax.numpy as jnp
from jax import lax
from jax.experimental import pallas as pl
from jax.experimental.pallas import tpu as pltpu
from jax.sharding import PartitionSpec as P

F32, BF16 = jnp.float32, jnp.bfloat16
SUBDOMS, HALF, FACES = 4, 4, 8
BLOCK, COLS, ORDER = 128, 384, 1024
ALL, SLOTS, COARSE = 32, 16, 128
OWN = COARSE // 16
N_SUB = 8
N_GRP = 16
UP = 8
TILE = 512
PER = TILE // BLOCK
MESH = pl.DeviceIdType.MESH
EXACT = lax.Precision.HIGHEST


def low(s, k):
    return s * FACES + HALF + k


def rows8(a):
    return jnp.sum(a.reshape(BLOCK // 8, 8, COLS), axis=0)


def one_row(acc):
    return jnp.sum(acc, axis=0, keepdims=True)


def mul(a, b):
    return jnp.dot(a, b, preferred_element_type=F32)


def mul_t(a, b):
    return lax.dot_general(a, b, (((0,), (0,)), ((), ())), preferred_element_type=F32)


def kernel(
    schur_h, mortar_h, load_h, coarse_h, partner, cmap, out,
    S, M, B, K, VB, Q, RB, TR, SU, AB, MT, TQ, SU2, RU2, RD2,
    OH, CR, CA, CX, RX, GX, AS, AG, AZ, INV,
    load_s, mort_s, schur_s, coarse_s,
    sd_s, sd_r, su_s, su_r, td_s, td_r, tu_s, tu_r,
    g_s, g_r, z_s, z_r,
):
    sub, grp = lax.axis_index("sub"), lax.axis_index("grp")
    above, below = (sub + 1) % N_SUB, (sub + N_SUB - 1) % N_SUB

    def in_group(d):
        return {"grp": (grp + d) % N_GRP}

    def over_sub(d):
        return {"sub": (sub + d) % N_SUB}

    def send(src, dst, ssem, rsem, device):
        return pltpu.make_async_remote_copy(
            src_ref=src, dst_ref=dst, send_sem=ssem, recv_sem=rsem,
            device_id=device, device_id_type=MESH,
        )

    def send_down(j):
        g = low(j // HALF, j % HALF)
        return send(TR.at[g], AB.at[j], sd_s.at[j], sd_r.at[j], {"sub": below})

    def send_up(j):
        return send(SU.at[j], MT.at[j], su_s.at[j], su_r.at[j], {"sub": above})

    def send_up2(j):
        return send(SU2.at[j], RU2.at[j], tu_s.at[j], tu_r.at[j], {"sub": above})

    def send_down2(j):
        g, i = low(j // HALF, j % HALF), j - UP
        return send(TQ.at[g], RD2.at[i], td_s.at[i], td_r.at[i], {"sub": below})

    def scatter_rows(p, d):
        to = (grp + d) % N_GRP
        return send(
            CX.at[p, to], RX.at[p, d - 1], g_s.at[p, 0, d - 1], g_r.at[p, 0, d - 1], in_group(d)
        )

    def gather_rows(p, d):
        return send(
            GX.at[p, grp], GX.at[p, grp], g_s.at[p, 1, d - 1], g_r.at[p, 1, d - 1], in_group(d)
        )

    def sum_grp(p, d):
        return send(
            AS.at[p, 0], AG.at[p, d - 1], g_s.at[p, 2, d - 1], g_r.at[p, 2, d - 1], in_group(d)
        )

    def sum_sub(p, d):
        return send(AS.at[p, 1], AZ.at[p, d - 1], z_s.at[p, d - 1], z_r.at[p, d - 1], over_sub(d))

    def start_all(copy, p, n):
        @pl.loop(1, n)
        def _(d):
            copy(p, d).start()

    def take_all(copy, p, n):
        @pl.loop(1, n)
        def _(d):
            copy(p, d).wait_recv()

    def end_all(copy, p, n):
        @pl.loop(1, n)
        def _(d):
            copy(p, d).wait_send()

    mort_c = pltpu.make_async_copy(mortar_h, M, mort_s)

    def load_c(s):
        span = pl.ds(s * FACES, FACES)
        return pltpu.make_async_copy(load_h.at[span], B.at[span], load_s.at[s])

    def schur_c(s):
        return pltpu.make_async_copy(schur_h.at[s], S.at[s], schur_s.at[s])

    coarse_c = pltpu.make_async_copy(coarse_h.at[0], K, coarse_s)
    for s in range(SUBDOMS):
        load_c(s).start()
    mort_c.start()
    coarse_c.start()
    for s in range(SUBDOMS):
        schur_c(s).start()

    barrier = pltpu.get_barrier_semaphore()

    @pl.loop(1, N_GRP)
    def _(d):
        pl.semaphore_signal(barrier, inc=1, device_id=in_group(d), device_id_type=MESH)

    @pl.loop(1, N_SUB)
    def _(d):
        pl.semaphore_signal(barrier, inc=1, device_id=over_sub(d), device_id_type=MESH)

    @pl.loop(0, SLOTS)
    def _(j):
        found = jnp.int32(0)
        for u in range(SLOTS):
            at = (u // HALF) * FACES + u % HALF
            found = jnp.where(partner[u // HALF, u % HALF] == j, at, found)
        INV[j] = found

    lanes = lax.broadcasted_iota(jnp.int32, (1, COARSE), 1)

    @pl.loop(0, SUBDOMS)
    def _(s):
        for c in range(FACES):
            OH[pl.ds(s * FACES + c, 1), :] = jnp.where(lanes == cmap[s, c], 1.0, 0.0).astype(F32)

    def coarse_start(p):
        local = lax.dot_general(
            OH[...], CR[...], (((0,), (0,)), ((), ())), precision=EXACT, preferred_element_type=F32
        )
        CX[p] = local.reshape(N_GRP, OWN, COLS)
        start_all(scatter_rows, p, N_GRP)

    def coarse_middle(p):
        take_all(scatter_rows, p, N_GRP)
        total = CX[p, grp]
        for d in range(1, N_GRP):
            total = total + RX[p, d - 1]
        GX[p, grp] = total
        start_all(gather_rows, p, N_GRP)

    def coarse_end(p):
        take_all(gather_rows, p, N_GRP)
        vector = GX[p].reshape(COARSE, COLS)
        value = jnp.dot(K[...], vector, precision=EXACT, preferred_element_type=F32)
        return value, one_row(jnp.sum((vector * value).reshape(N_GRP, 8, COLS), axis=0))

    for s in range(SUBDOMS):
        load_c(s).wait()

    @pl.loop(0, SUBDOMS)
    def _(s):
        for f in range(FACES):
            g = s * FACES + f
            CR[pl.ds(g, 1), :] = B[g, 0:1, :]

    pl.semaphore_wait(barrier, N_GRP + N_SUB - 2)
    coarse_start(0)
    mort_c.wait()

    def first_low(i, acc):
        s = SUBDOMS - 1 - i
        for k in reversed(range(HALF)):
            j, g = s * HALF + k, low(s, k)
            b = B[g]
            acc = acc + rows8(b * b)
            half = b.astype(BF16)
            VB[g] = half
            TR[g] = mul(M[g], half).astype(BF16)
            send_down(j).start()
        return acc

    def first_up(s, acc):
        for k in range(HALF):
            g = s * FACES + k
            b = B[g]
            acc = acc + rows8(b * b)
            half = b.astype(BF16)
            VB[g] = half
            TR[g] = mul(M[g], half).astype(BF16)
        return acc

    zero8 = jnp.zeros((8, COLS), F32)
    acc0 = lax.fori_loop(0, SUBDOMS, first_up, zero8)

    @pl.loop(0, SLOTS)
    def _(j):
        SU[j] = TR[INV[j]]
        send_up(j).start()

    acc0 = lax.fori_loop(0, SUBDOMS, first_low, acc0)

    def stiff(s, acc):
        schur_c(s).wait()
        field = VB[s * FACES : (s + 1) * FACES].reshape(ORDER, COLS)

        def tile(i, acc):
            part = mul(S[s, pl.ds(pl.multiple_of(i * TILE, TILE), TILE), :], field)
            for t in range(PER):
                g = s * FACES + i * PER + t
                q = part[t * BLOCK : (t + 1) * BLOCK]
                Q[g] = q
                acc = acc + rows8(B[g] * q)
            return acc

        return lax.fori_loop(0, ORDER // TILE, tile, acc)

    acc1 = stiff(0, zero8)
    acc1 = stiff(1, acc1)
    coarse_c.wait()
    coarse_middle(0)
    acc1 = stiff(2, acc1)
    acc1 = stiff(3, acc1)

    def jump2(own, mate):
        d = (own.astype(F32) - mate.astype(F32)).astype(BF16).astype(F32)
        return rows8(d * d)

    def count_low(j, acc):
        send_up(j).wait_recv()
        return acc + jump2(TR[low(j // HALF, j % HALF)], MT[j])

    def count_up(i, acc):
        j = SLOTS - 1 - i
        send_down(j).wait_recv()
        return acc + jump2(TR[INV[j]], AB[j])

    acc1 = lax.fori_loop(0, UP, count_low, acc1)
    acc1 = lax.fori_loop(0, SLOTS - UP, count_up, acc1)

    def sum_start(p, values):
        for i, v in enumerate(values):
            AS[p, 0, i : i + 1, :] = one_row(v)
        AS[p, 0, len(values) : 8, :] = jnp.zeros((8 - len(values), COLS), F32)
        start_all(sum_grp, p, N_GRP)

    def sum_middle(p, row, extra):
        take_all(sum_grp, p, N_GRP)
        total = AS[p, 0]
        for d in range(1, N_GRP):
            total = total + AG[p, d - 1]
        AS[p, 1] = total
        AS[p, 1, row : row + 1, :] = AS[p, 1, row : row + 1, :] + extra
        start_all(sum_sub, p, N_SUB)

    def sum_end(p):
        take_all(sum_sub, p, N_SUB)
        total = AS[p, 1]
        for d in range(1, N_SUB):
            total = total + AZ[p, d - 1]
        return total

    sum_start(0, [acc0, acc1])
    coarse_val, coarse_energy = coarse_end(0)
    CA[...] = jnp.dot(OH[...], coarse_val, precision=EXACT, preferred_element_type=F32)

    @pl.loop(0, SUBDOMS)
    def _(s):
        for f in range(FACES):
            g = s * FACES + f
            Q[g, 0:1, :] = Q[g, 0:1, :] + CA[pl.ds(g, 1), :]

    def finish(g, mate):
        jump = (TR[g].astype(F32) - mate.astype(F32)).astype(BF16)
        Q[g] = Q[g] + mul_t(M[g], jump)

    def lower(s, wait):
        for k in range(HALF):
            if wait:
                send_up(s * HALF + k).wait_recv()
            finish(low(s, k), MT[s * HALF + k])

    @pl.loop(0, UP // HALF)
    def _(s):
        lower(s, False)

    sum_middle(0, 1, coarse_energy)

    @pl.loop(UP // HALF, SUBDOMS)
    def _(s):
        lower(s, True)

    @pl.loop(0, UP)
    def _(j):
        send_down(j).wait_recv()

    @pl.loop(0, SUBDOMS)
    def _(s):
        for k in range(HALF):
            finish(s * FACES + k, AB[partner[s, k]])

    sums = sum_end(0)
    norm0, curve0 = sums[0:1], sums[1:2]
    step0 = norm0 / curve0

    @pl.loop(0, SUBDOMS)
    def _(s):
        for f in range(FACES):
            g = s * FACES + f
            CR[pl.ds(g, 1), :] = B[g, 0:1, :] - step0 * Q[g, 0:1, :]

    coarse_start(1)

    def resid(g, carry):
        n1, gq = carry
        q = Q[g]
        r = B[g] - step0 * q
        half = r.astype(BF16)
        Q[g] = r
        RB[g] = half
        TQ[g] = mul(M[g], half).astype(BF16)
        return n1 + rows8(r * r), gq + rows8(r * q)

    def resid_up(s, carry):
        for k in range(HALF):
            carry = resid(s * FACES + k, carry)
        return carry

    def resid_low(s, carry):
        for k in range(HALF):
            carry = resid(low(s, k), carry)
        return carry

    def resid_low_send(s, carry):
        for k in range(HALF):
            carry = resid(low(s, k), carry)
            send_down2(s * HALF + k).start()
        return carry

    carry = lax.fori_loop(UP // HALF, SUBDOMS, resid_low_send, (zero8, zero8))
    carry = lax.fori_loop(0, SUBDOMS, resid_up, carry)

    @pl.loop(0, UP)
    def _(j):
        SU2[j] = TQ[INV[j]]
        send_up2(j).start()

    acc_n, acc_g = lax.fori_loop(0, UP // HALF, resid_low, carry)

    def inner(s, acc):
        field = RB[s * FACES : (s + 1) * FACES].reshape(ORDER, COLS)

        def tile(i, acc):
            part = mul(S[s, pl.ds(pl.multiple_of(i * TILE, TILE), TILE), :], field)
            for t in range(PER):
                acc = acc + rows8(Q[s * FACES + i * PER + t] * part[t * BLOCK : (t + 1) * BLOCK])
            return acc

        return lax.fori_loop(0, ORDER // TILE, tile, acc)

    energy = inner(0, zero8)
    energy = inner(1, energy)
    energy = inner(2, energy)
    coarse_middle(1)
    energy = inner(3, energy)

    def pair2(own, mate):
        d = own.astype(F32) - mate.astype(F32)
        return rows8(d * d)

    def pair_low(j, acc):
        send_up2(j).wait_recv()
        return acc + pair2(TQ[low(j // HALF, j % HALF)], RU2[j])

    def pair_up(j, acc):
        send_down2(j).wait_recv()
        return acc + pair2(TQ[INV[j]], RD2[j - UP])

    energy = lax.fori_loop(UP, SLOTS, pair_up, energy)
    energy = lax.fori_loop(0, UP, pair_low, energy)

    sum_start(1, [acc_n, acc_g, energy])
    _, coarse_energy = coarse_end(1)
    sum_middle(1, 2, coarse_energy)

    @pl.loop(0, SLOTS)
    def _(j):
        send_down(j).wait_send()
        send_up(j).wait_send()

    @pl.loop(0, UP)
    def _(j):
        send_up2(j).wait_send()

    @pl.loop(UP, SLOTS)
    def _(j):
        send_down2(j).wait_send()

    for p in range(2):
        end_all(scatter_rows, p, N_GRP)
        end_all(gather_rows, p, N_GRP)
        end_all(sum_grp, p, N_GRP)
    end_all(sum_sub, 0, N_SUB)

    sums = sum_end(1)
    norm1, cross, energy1 = sums[0:1], sums[1:2], sums[2:3]
    beta = norm1 / norm0
    curve1 = energy1 + 2.0 * beta * cross + beta * beta * curve0
    step1 = norm1 / curve1
    with_load = step0 + step1 * beta

    @pl.loop(0, SUBDOMS)
    def _(s):
        for f in range(FACES):
            g = s * FACES + f
            out[g] = with_load * B[g] + step1 * Q[g]

    end_all(sum_sub, 1, N_SUB)


def on_device(schur, mortar, partner, corner_map, coarse_inv, load):
    vm, dma = pltpu.VMEM, pltpu.SemaphoreType.DMA
    anywhere = pl.BlockSpec(memory_space=pl.ANY)
    scalar = pl.BlockSpec(memory_space=pltpu.SMEM)
    faces_half = (ALL, BLOCK, COLS)
    slots_half = (SLOTS, BLOCK, COLS)
    scratch = [
        vm((SUBDOMS, ORDER, ORDER), BF16),
        vm((ALL, BLOCK, BLOCK), BF16),
        vm(faces_half, F32),
        vm((COARSE, COARSE), F32),
        vm(faces_half, BF16),
        vm(faces_half, F32),
        vm(faces_half, BF16),
        vm(faces_half, BF16),
        vm(slots_half, BF16),
        vm(slots_half, BF16),
        vm(slots_half, BF16),
        vm(faces_half, BF16),
        vm((UP, BLOCK, COLS), BF16),
        vm((UP, BLOCK, COLS), BF16),
        vm((SLOTS - UP, BLOCK, COLS), BF16),
        vm((ALL, COARSE), F32),
        vm((ALL, COLS), F32),
        vm((ALL, COLS), F32),
        vm((2, N_GRP, OWN, COLS), F32),
        vm((2, N_GRP - 1, OWN, COLS), F32),
        vm((2, N_GRP, OWN, COLS), F32),
        vm((2, 2, 8, COLS), F32),
        vm((2, N_GRP - 1, 8, COLS), F32),
        vm((2, N_SUB - 1, 8, COLS), F32),
        pltpu.SMEM((SLOTS,), jnp.int32),
        dma((SUBDOMS,)), dma, dma((SUBDOMS,)), dma,
        dma((SLOTS,)), dma((SLOTS,)), dma((SLOTS,)), dma((SLOTS,)),
        dma((SLOTS - UP,)), dma((SLOTS - UP,)), dma((UP,)), dma((UP,)),
        dma((2, 3, N_GRP - 1)), dma((2, 3, N_GRP - 1)),
        dma((2, N_SUB - 1)), dma((2, N_SUB - 1)),
    ]
    out = pl.pallas_call(
        kernel,
        out_shape=pltpu.VMEM(faces_half, F32),
        in_specs=[anywhere] * 4 + [scalar] * 2,
        out_specs=pl.BlockSpec(memory_space=pltpu.VMEM),
        scratch_shapes=scratch,
        compiler_params=pltpu.CompilerParams(
            collective_id=0, has_side_effects=True, vmem_limit_bytes=50 * 1024 * 1024
        ),
    )(
        schur,
        mortar.reshape(ALL, BLOCK, BLOCK),
        load.reshape(ALL, BLOCK, COLS),
        coarse_inv,
        partner,
        corner_map,
    )
    return out.reshape(SUBDOMS, ORDER, COLS)


def solution(mesh):
    return jax.shard_map(
        on_device,
        mesh=mesh,
        in_specs=(
            P(("sub", "grp"), None, None),
            P(("sub", "grp"), None, None, None),
            P(("sub", "grp"), None),
            P(("sub", "grp"), None),
            P("sub", None, None),
            P(("sub", "grp"), None, None),
        ),
        out_specs=P(("sub", "grp"), None, None),
        check_vma=False,
    )
```

```python
import functools

import jax
import jax.numpy as jnp
from jax import lax
from jax.experimental import pallas as pl
from jax.experimental.pallas import tpu as pltpu
from jax.sharding import PartitionSpec as P

F32, BF16 = jnp.float32, jnp.bfloat16
SUBDOMS, HALF, FACES = 4, 4, 8
BLOCK, COLS, ORDER = 128, 384, 1024
ALL, SLOTS, COARSE = 32, 16, 128
OWN = COARSE // 16
N_SUB = 8
N_GRP = 16
UP = 8
TILE = 1024
PER = TILE // BLOCK
MESH = pl.DeviceIdType.MESH
EXACT = lax.Precision.HIGHEST


def low(s, k):
    return s * FACES + HALF + k


def rows8(a):
    return jnp.sum(a.reshape(BLOCK // 8, 8, COLS), axis=0)


def one_row(acc):
    return jnp.sum(acc, axis=0, keepdims=True)


def mul(a, b):
    return jnp.dot(a, b, preferred_element_type=F32)


def mul_t(a, b):
    return lax.dot_general(a, b, (((0,), (0,)), ((), ())), preferred_element_type=F32)


def kernel(
    schur_h, mortar_h, load_h, coarse_h, partner, cmap, B, Q, COEF,
    S, M, K, VB, RB, TR, SU, AB, MT, PP, TQ, TU, SU2, RU2, RD2,
    OH, CR, CA, CX, RX, GX, AS, AG, AZ, INV,
    load_s, mort_s, schur_s, coarse_s,
    sd_s, sd_r, su_s, su_r, td_s, td_r, tu_s, tu_r,
    g_s, g_r, z_s, z_r,
):
    sub, grp = lax.axis_index("sub"), lax.axis_index("grp")
    above, below = (sub + 1) % N_SUB, (sub + N_SUB - 1) % N_SUB

    def in_group(d):
        return {"grp": (grp + d) % N_GRP}

    def over_sub(d):
        return {"sub": (sub + d) % N_SUB}

    def send(src, dst, ssem, rsem, device):
        return pltpu.make_async_remote_copy(
            src_ref=src, dst_ref=dst, send_sem=ssem, recv_sem=rsem,
            device_id=device, device_id_type=MESH,
        )

    def send_down(j):
        g = low(j // HALF, j % HALF)
        return send(TR.at[g], AB.at[j], sd_s.at[j], sd_r.at[j], {"sub": below})

    def send_up(j):
        return send(SU.at[j], MT.at[j], su_s.at[j], su_r.at[j], {"sub": above})

    def send_up2(j):
        return send(SU2.at[j], RU2.at[j], tu_s.at[j], tu_r.at[j], {"sub": above})

    def send_down2(j):
        g, i = low(j // HALF, j % HALF), j - UP
        return send(TQ.at[g], RD2.at[i], td_s.at[i], td_r.at[i], {"sub": below})

    def scatter_rows(p, d):
        to = (grp + d) % N_GRP
        return send(
            CX.at[p, to], RX.at[p, d - 1], g_s.at[p, 0, d - 1], g_r.at[p, 0, d - 1], in_group(d)
        )

    def gather_rows(p, d):
        return send(
            GX.at[p, grp], GX.at[p, grp], g_s.at[p, 1, d - 1], g_r.at[p, 1, d - 1], in_group(d)
        )

    def sum_grp(p, d):
        return send(
            AS.at[p, 0], AG.at[p, d - 1], g_s.at[p, 2, d - 1], g_r.at[p, 2, d - 1], in_group(d)
        )

    def sum_sub(p, d):
        return send(AS.at[p, 1], AZ.at[p, d - 1], z_s.at[p, d - 1], z_r.at[p, d - 1], over_sub(d))

    def start_all(copy, p, n):
        @pl.loop(1, n)
        def _(d):
            copy(p, d).start()

    def take_all(copy, p, n):
        @pl.loop(1, n)
        def _(d):
            copy(p, d).wait_recv()

    def end_all(copy, p, n):
        @pl.loop(1, n)
        def _(d):
            copy(p, d).wait_send()

    barrier = pltpu.get_barrier_semaphore()

    @pl.loop(1, N_GRP)
    def _(d):
        pl.semaphore_signal(barrier, inc=1, device_id=in_group(d), device_id_type=MESH)

    @pl.loop(1, N_SUB)
    def _(d):
        pl.semaphore_signal(barrier, inc=1, device_id=over_sub(d), device_id_type=MESH)

    mort_c = pltpu.make_async_copy(mortar_h, M, mort_s)

    def load_c(s):
        span = pl.ds(s * FACES, FACES)
        return pltpu.make_async_copy(load_h.at[span], B.at[span], load_s.at[s])

    def schur_c(s):
        return pltpu.make_async_copy(schur_h.at[s], S.at[s], schur_s.at[s])

    coarse_c = pltpu.make_async_copy(coarse_h.at[0], K, coarse_s)
    mort_c.start()
    for s in range(SUBDOMS):
        load_c(s).start()
    coarse_c.start()

    @pl.loop(0, SLOTS)
    def _(j):
        found = jnp.int32(0)
        for u in range(SLOTS):
            at = (u // HALF) * FACES + u % HALF
            found = jnp.where(partner[u // HALF, u % HALF] == j, at, found)
        INV[j] = found

    lanes = lax.broadcasted_iota(jnp.int32, (1, COARSE), 1)

    @pl.loop(0, SUBDOMS)
    def _(s):
        for c in range(FACES):
            OH[pl.ds(s * FACES + c, 1), :] = jnp.where(lanes == cmap[s, c], 1.0, 0.0).astype(F32)

    def coarse_start(p):
        local = lax.dot_general(
            OH[...], CR[...], (((0,), (0,)), ((), ())), precision=EXACT, preferred_element_type=F32
        )
        CX[p] = local.reshape(N_GRP, OWN, COLS)
        start_all(scatter_rows, p, N_GRP)

    def coarse_middle(p):
        take_all(scatter_rows, p, N_GRP)
        total = CX[p, grp]
        for d in range(1, N_GRP):
            total = total + RX[p, d - 1]
        GX[p, grp] = total
        start_all(gather_rows, p, N_GRP)

    def coarse_end(p, step):
        take_all(gather_rows, p, N_GRP)
        vector = GX[0].reshape(COARSE, COLS)
        if p == 1:
            vector = vector - step * GX[1].reshape(COARSE, COLS)
        value = jnp.dot(K[...], vector, precision=EXACT, preferred_element_type=F32)
        return value, one_row(jnp.sum((vector * value).reshape(N_GRP, 8, COLS), axis=0))

    def first(g, acc):
        b = B[g]
        half = b.astype(BF16)
        VB[g] = half
        TR[g] = mul(M[g], half).astype(BF16)
        return acc + rows8(b * b)

    def first_up(s, acc):
        load_c(s).wait()
        for k in range(HALF):
            acc = first(s * FACES + k, acc)
        return acc

    zero8 = jnp.zeros((8, COLS), F32)
    mort_c.wait()
    acc0 = lax.fori_loop(0, SUBDOMS, first_up, zero8)
    for s in range(SUBDOMS):
        schur_c(s).start()
    pl.semaphore_wait(barrier, N_GRP + N_SUB - 2)

    def first_low(i, acc):
        for k in range(HALF):
            up = i * HALF + k
            SU[up] = TR[INV[up]]
            send_up(up).start()
            s, t = SUBDOMS - 1 - i, HALF - 1 - k
            acc = first(low(s, t), acc)
            send_down(s * HALF + t).start()
        return acc

    acc0 = lax.fori_loop(0, SUBDOMS, first_low, acc0)

    @pl.loop(0, SUBDOMS)
    def _(s):
        for f in range(FACES):
            g = s * FACES + f
            CR[pl.ds(g, 1), :] = B[g, 0:1, :]

    coarse_start(0)

    def stiff(s, acc):
        schur_c(s).wait()
        field = VB[s * FACES : (s + 1) * FACES].reshape(ORDER, COLS)

        def tile(i, acc):
            part = mul(S[s, pl.ds(pl.multiple_of(i * TILE, TILE), TILE), :], field)
            for t in range(PER):
                g = s * FACES + i * PER + t
                q = part[t * BLOCK : (t + 1) * BLOCK]
                Q[g] = q
                acc = acc + rows8(B[g] * q)
            return acc

        return lax.fori_loop(0, ORDER // TILE, tile, acc)

    acc1 = stiff(0, zero8)
    acc1 = stiff(1, acc1)
    acc1 = stiff(2, acc1)
    acc1 = stiff(3, acc1)
    coarse_c.wait()
    coarse_middle(0)

    def jump_of(own, mate):
        return (own.astype(F32) - mate.astype(F32)).astype(BF16)

    def square(jump):
        d = jump.astype(F32)
        return rows8(d * d)

    def pull(i):
        send_up(i).wait_recv()
        g = low(i // HALF, i % HALF)
        jump_l = jump_of(TR[g], MT[i])
        Q[g] = Q[g] + mul_t(M[g], jump_l)
        j = SLOTS - 1 - i
        send_down(j).wait_recv()
        g = INV[j]
        jump_u = jump_of(TR[g], AB[j])
        PP[j] = mul_t(M[g], jump_u)
        return jump_l, jump_u

    def pull_count(i, acc):
        jump_l, jump_u = pull(i)
        return acc + square(jump_l) + square(jump_u)

    acc1 = lax.fori_loop(0, UP, pull_count, acc1)

    def sum_start(p, values):
        for i, v in enumerate(values):
            AS[p, 0, i : i + 1, :] = one_row(v)
        AS[p, 0, len(values) : 8, :] = jnp.zeros((8 - len(values), COLS), F32)
        start_all(sum_grp, p, N_GRP)

    def sum_middle(p, row, extra):
        take_all(sum_grp, p, N_GRP)
        total = AS[p, 0]
        for d in range(1, N_GRP):
            total = total + AG[p, d - 1]
        AS[p, 1] = total
        AS[p, 1, row : row + 1, :] = AS[p, 1, row : row + 1, :] + extra
        start_all(sum_sub, p, N_SUB)

    def sum_end(p):
        take_all(sum_sub, p, N_SUB)
        total = AS[p, 1]
        for d in range(1, N_SUB):
            total = total + AZ[p, d - 1]
        return total

    sum_start(0, [acc0, acc1])
    coarse_val, coarse_energy = coarse_end(0, None)
    CA[...] = jnp.dot(OH[...], coarse_val, precision=EXACT, preferred_element_type=F32)

    @pl.loop(0, SUBDOMS)
    def _(s):
        for f in range(FACES):
            g = s * FACES + f
            Q[g, 0:1, :] = Q[g, 0:1, :] + CA[pl.ds(g, 1), :]

    @pl.loop(UP, 12)
    def _(i):
        pull(i)

    sum_middle(0, 1, coarse_energy)

    @pl.loop(12, SLOTS)
    def _(i):
        pull(i)

    def image_send(i, none):
        j = UP + i
        g = low(j // HALF, j % HALF)
        TQ[g] = mul(M[g], Q[g].astype(BF16)).astype(BF16)
        send_down2(j).start()
        g = INV[i]
        SU2[i] = mul(M[g], (Q[g] + PP[i]).astype(BF16)).astype(BF16)
        send_up2(i).start()
        return none

    lax.fori_loop(0, UP, image_send, 0)

    @pl.loop(0, SUBDOMS)
    def _(s):
        for f in range(FACES):
            g = s * FACES + f
            row = Q[g, 0:1, :]
            if f < HALF:
                row = row + PP[partner[s, f], 0:1, :]
            CR[pl.ds(g, 1), :] = row

    coarse_start(1)

    @pl.loop(0, UP)
    def _(i):
        g = low(i // HALF, i % HALF)
        TQ[g] = mul(M[g], Q[g].astype(BF16)).astype(BF16)
        g = INV[UP + i]
        TU[i] = mul(M[g], (Q[g] + PP[UP + i]).astype(BF16)).astype(BF16)

    sums = sum_end(0)
    norm0, curve0 = sums[0:1], sums[1:2]
    step0 = norm0 / curve0

    def resid(s, carry):
        n1, gq = carry
        for f in range(FACES):
            g = s * FACES + f
            q = Q[g]
            if f < HALF:
                q = q + PP[partner[s, f]]
            r = B[g] - step0 * q
            Q[g] = r
            RB[g] = r.astype(BF16)
            n1, gq = n1 + rows8(r * r), gq + rows8(r * q)
        return n1, gq

    acc_n, acc_g = lax.fori_loop(0, SUBDOMS, resid, (zero8, zero8))

    def inner(s, acc):
        field = RB[s * FACES : (s + 1) * FACES].reshape(ORDER, COLS)

        def tile(i, acc):
            part = mul(S[s, pl.ds(pl.multiple_of(i * TILE, TILE), TILE), :], field)
            for t in range(PER):
                acc = acc + rows8(Q[s * FACES + i * PER + t] * part[t * BLOCK : (t + 1) * BLOCK])
            return acc

        return lax.fori_loop(0, ORDER // TILE, tile, acc)

    energy = inner(0, zero8)
    energy = inner(1, energy)
    coarse_middle(1)
    energy = inner(2, energy)
    energy = inner(3, energy)

    def pair2(first_jump, own, mate):
        d = first_jump.astype(F32) - step0 * (own.astype(F32) - mate.astype(F32))
        return rows8(d * d)

    def pair_low(j, acc):
        send_up2(j).wait_recv()
        g = low(j // HALF, j % HALF)
        return acc + pair2(jump_of(TR[g], MT[j]), TQ[g], RU2[j])

    def pair_up(j, acc):
        send_down2(j).wait_recv()
        g = INV[j]
        return acc + pair2(jump_of(TR[g], AB[j]), TU[j - UP], RD2[j - UP])

    energy = lax.fori_loop(UP, SLOTS, pair_up, energy)
    energy = lax.fori_loop(0, UP, pair_low, energy)

    sum_start(1, [acc_n, acc_g, energy])
    _, coarse_energy = coarse_end(1, step0)
    sum_middle(1, 2, coarse_energy)

    @pl.loop(0, SLOTS)
    def _(j):
        send_down(j).wait_send()
        send_up(j).wait_send()

    @pl.loop(0, UP)
    def _(j):
        send_up2(j).wait_send()

    @pl.loop(UP, SLOTS)
    def _(j):
        send_down2(j).wait_send()

    for p in range(2):
        end_all(scatter_rows, p, N_GRP)
        end_all(gather_rows, p, N_GRP)
        end_all(sum_grp, p, N_GRP)
    end_all(sum_sub, 0, N_SUB)

    sums = sum_end(1)
    norm1, cross, energy1 = sums[0:1], sums[1:2], sums[2:3]
    beta = norm1 / norm0
    curve1 = energy1 + 2.0 * beta * cross + beta * beta * curve0
    step1 = norm1 / curve1
    with_load = step0 + step1 * beta

    COEF[0:1, :] = with_load
    COEF[1:2, :] = step1
    COEF[2:8, :] = jnp.zeros((6, COLS), F32)
    end_all(sum_sub, 1, N_SUB)


def on_device(schur, mortar, partner, corner_map, coarse_inv, load):
    vm, dma = pltpu.VMEM, pltpu.SemaphoreType.DMA
    anywhere = pl.BlockSpec(memory_space=pl.ANY)
    scalar = pl.BlockSpec(memory_space=pltpu.SMEM)
    faces_half = (ALL, BLOCK, COLS)
    slots_half = (SLOTS, BLOCK, COLS)
    scratch = [
        vm((SUBDOMS, ORDER, ORDER), BF16),
        vm((ALL, BLOCK, BLOCK), BF16),
        vm((COARSE, COARSE), F32),
        vm(faces_half, BF16),
        vm(faces_half, BF16),
        vm(faces_half, BF16),
        vm(slots_half, BF16),
        vm(slots_half, BF16),
        vm(slots_half, BF16),
        vm(slots_half, F32),
        vm(faces_half, BF16),
        vm((SLOTS - UP, BLOCK, COLS), BF16),
        vm((UP, BLOCK, COLS), BF16),
        vm((UP, BLOCK, COLS), BF16),
        vm((SLOTS - UP, BLOCK, COLS), BF16),
        vm((ALL, COARSE), F32),
        vm((ALL, COLS), F32),
        vm((ALL, COLS), F32),
        vm((2, N_GRP, OWN, COLS), F32),
        vm((2, N_GRP - 1, OWN, COLS), F32),
        vm((2, N_GRP, OWN, COLS), F32),
        vm((2, 2, 8, COLS), F32),
        vm((2, N_GRP - 1, 8, COLS), F32),
        vm((2, N_SUB - 1, 8, COLS), F32),
        pltpu.SMEM((SLOTS,), jnp.int32),
        dma((SUBDOMS,)), dma, dma((SUBDOMS,)), dma,
        dma((SLOTS,)), dma((SLOTS,)), dma((SLOTS,)), dma((SLOTS,)),
        dma((SLOTS - UP,)), dma((SLOTS - UP,)), dma((UP,)), dma((UP,)),
        dma((2, 3, N_GRP - 1)), dma((2, 3, N_GRP - 1)),
        dma((2, N_SUB - 1)), dma((2, N_SUB - 1)),
    ]
    loads, residual, coef = pl.pallas_call(
        kernel,
        out_shape=[vm(faces_half, F32), vm(faces_half, F32), vm((8, COLS), F32)],
        in_specs=[anywhere] * 4 + [scalar] * 2,
        out_specs=[pl.BlockSpec(memory_space=pltpu.VMEM)] * 3,
        scratch_shapes=scratch,
        compiler_params=pltpu.CompilerParams(
            collective_id=0, has_side_effects=True, vmem_limit_bytes=46 * 1024 * 1024
        ),
    )(
        schur,
        mortar.reshape(ALL, BLOCK, BLOCK),
        load.reshape(ALL, BLOCK, COLS),
        coarse_inv,
        partner,
        corner_map,
    )
    out = coef[0] * loads + coef[1] * residual
    return out.reshape(SUBDOMS, ORDER, COLS)


def solution(mesh):
    return jax.shard_map(
        on_device,
        mesh=mesh,
        in_specs=(
            P(("sub", "grp"), None, None),
            P(("sub", "grp"), None, None, None),
            P(("sub", "grp"), None),
            P(("sub", "grp"), None),
            P("sub", None, None),
            P(("sub", "grp"), None, None),
        ),
        out_specs=P(("sub", "grp"), None, None),
        check_vma=False,
    )
```

```python
import functools

import jax
import jax.numpy as jnp
from jax import lax
from jax.experimental import pallas as pl
from jax.experimental.pallas import tpu as pltpu
from jax.sharding import PartitionSpec as P

F32, BF16 = jnp.float32, jnp.bfloat16
SUBDOMS, HALF, FACES = 4, 4, 8
BLOCK, COLS, ORDER = 128, 384, 1024
ALL, SLOTS, COARSE = 32, 16, 128
OWN = COARSE // 16
N_SUB = 8
N_GRP = 16
UP = 8
TILE = 1024
PER = TILE // BLOCK
MESH = pl.DeviceIdType.MESH
EXACT = lax.Precision.HIGHEST


def low(s, k):
    return s * FACES + HALF + k


def rows8(a):
    return jnp.sum(a.reshape(BLOCK // 8, 8, COLS), axis=0)


def one_row(acc):
    return jnp.sum(acc, axis=0, keepdims=True)


def mul(a, b):
    return jnp.dot(a, b, preferred_element_type=F32)


def mul_t(a, b):
    return lax.dot_general(a, b, (((0,), (0,)), ((), ())), preferred_element_type=F32)


def kernel(
    schur_h, mortar_h, load_h, coarse_h, partner, cmap, Q,
    S, M, B, K, VB, RB, TR, SU, AB, MT, PP, TQ, TU, SU2, RU2, RD2,
    OH, CR, CA, CX, RX, GX, AS, AG, AZ, INV,
    load_s, mort_s, schur_s, coarse_s,
    sd_s, sd_r, su_s, su_r, td_s, td_r, tu_s, tu_r,
    g_s, g_r, z_s, z_r,
):
    sub, grp = lax.axis_index("sub"), lax.axis_index("grp")
    above, below = (sub + 1) % N_SUB, (sub + N_SUB - 1) % N_SUB

    def in_group(d):
        return {"grp": (grp + d) % N_GRP}

    def over_sub(d):
        return {"sub": (sub + d) % N_SUB}

    def send(src, dst, ssem, rsem, device):
        return pltpu.make_async_remote_copy(
            src_ref=src, dst_ref=dst, send_sem=ssem, recv_sem=rsem,
            device_id=device, device_id_type=MESH,
        )

    def send_down(j):
        g = low(j // HALF, j % HALF)
        return send(TR.at[g], AB.at[j], sd_s.at[j], sd_r.at[j], {"sub": below})

    def send_up(j):
        return send(SU.at[j], MT.at[j], su_s.at[j], su_r.at[j], {"sub": above})

    def send_up2(j):
        return send(SU2.at[j], RU2.at[j], tu_s.at[j], tu_r.at[j], {"sub": above})

    def send_down2(j):
        g, i = low(j // HALF, j % HALF), j - UP
        return send(TQ.at[g], RD2.at[i], td_s.at[i], td_r.at[i], {"sub": below})

    def scatter_rows(p, d):
        to = (grp + d) % N_GRP
        return send(
            CX.at[p, to], RX.at[p, d - 1], g_s.at[p, 0, d - 1], g_r.at[p, 0, d - 1], in_group(d)
        )

    def gather_rows(p, d):
        return send(
            GX.at[p, grp], GX.at[p, grp], g_s.at[p, 1, d - 1], g_r.at[p, 1, d - 1], in_group(d)
        )

    def sum_grp(p, d):
        return send(
            AS.at[p, 0], AG.at[p, d - 1], g_s.at[p, 2, d - 1], g_r.at[p, 2, d - 1], in_group(d)
        )

    def sum_sub(p, d):
        return send(AS.at[p, 1], AZ.at[p, d - 1], z_s.at[p, d - 1], z_r.at[p, d - 1], over_sub(d))

    def start_all(copy, p, n):
        @pl.loop(1, n)
        def _(d):
            copy(p, d).start()

    def take_all(copy, p, n):
        @pl.loop(1, n)
        def _(d):
            copy(p, d).wait_recv()

    def end_all(copy, p, n):
        @pl.loop(1, n)
        def _(d):
            copy(p, d).wait_send()

    barrier = pltpu.get_barrier_semaphore()

    @pl.loop(1, N_GRP)
    def _(d):
        pl.semaphore_signal(barrier, inc=1, device_id=in_group(d), device_id_type=MESH)

    @pl.loop(1, N_SUB)
    def _(d):
        pl.semaphore_signal(barrier, inc=1, device_id=over_sub(d), device_id_type=MESH)

    mort_c = pltpu.make_async_copy(mortar_h, M, mort_s)

    def load_c(s):
        span = pl.ds(s * FACES, FACES)
        return pltpu.make_async_copy(load_h.at[span], B.at[span], load_s.at[s])

    def schur_c(s):
        return pltpu.make_async_copy(schur_h.at[s], S.at[s], schur_s.at[s])

    coarse_c = pltpu.make_async_copy(coarse_h.at[0], K, coarse_s)
    mort_c.start()
    for s in range(SUBDOMS):
        load_c(s).start()
    coarse_c.start()

    @pl.loop(0, SLOTS)
    def _(j):
        found = jnp.int32(0)
        for u in range(SLOTS):
            at = (u // HALF) * FACES + u % HALF
            found = jnp.where(partner[u // HALF, u % HALF] == j, at, found)
        INV[j] = found

    lanes = lax.broadcasted_iota(jnp.int32, (1, COARSE), 1)

    @pl.loop(0, SUBDOMS)
    def _(s):
        for c in range(FACES):
            OH[pl.ds(s * FACES + c, 1), :] = jnp.where(lanes == cmap[s, c], 1.0, 0.0).astype(F32)

    def coarse_start(p):
        local = lax.dot_general(
            OH[...], CR[...], (((0,), (0,)), ((), ())), precision=EXACT, preferred_element_type=F32
        )
        CX[p] = local.reshape(N_GRP, OWN, COLS)
        start_all(scatter_rows, p, N_GRP)

    def coarse_middle(p):
        take_all(scatter_rows, p, N_GRP)
        total = CX[p, grp]
        for d in range(1, N_GRP):
            total = total + RX[p, d - 1]
        GX[p, grp] = total
        start_all(gather_rows, p, N_GRP)

    def coarse_end(p, step):
        take_all(gather_rows, p, N_GRP)
        vector = GX[0].reshape(COARSE, COLS)
        if p == 1:
            vector = vector - step * GX[1].reshape(COARSE, COLS)
        value = jnp.dot(K[...], vector, precision=EXACT, preferred_element_type=F32)
        return value, one_row(jnp.sum((vector * value).reshape(N_GRP, 8, COLS), axis=0))

    def first(g, acc):
        b = B[g]
        half = b.astype(BF16)
        VB[g] = half
        TR[g] = mul(M[g], half).astype(BF16)
        return acc + rows8(b * b)

    def first_up(s, acc):
        load_c(s).wait()
        for k in range(HALF):
            acc = first(s * FACES + k, acc)
        return acc

    zero8 = jnp.zeros((8, COLS), F32)
    mort_c.wait()
    acc0 = lax.fori_loop(0, SUBDOMS, first_up, zero8)
    for s in range(SUBDOMS):
        schur_c(s).start()
    pl.semaphore_wait(barrier, N_GRP + N_SUB - 2)

    def first_low(i, acc):
        for k in range(HALF):
            up = i * HALF + k
            SU[up] = TR[INV[up]]
            send_up(up).start()
            s, t = SUBDOMS - 1 - i, HALF - 1 - k
            acc = first(low(s, t), acc)
            send_down(s * HALF + t).start()
        return acc

    acc0 = lax.fori_loop(0, SUBDOMS, first_low, acc0)

    @pl.loop(0, SUBDOMS)
    def _(s):
        for f in range(FACES):
            g = s * FACES + f
            CR[pl.ds(g, 1), :] = B[g, 0:1, :]

    coarse_start(0)

    def stiff(s, acc):
        schur_c(s).wait()
        field = VB[s * FACES : (s + 1) * FACES].reshape(ORDER, COLS)

        def tile(i, acc):
            part = mul(S[s, pl.ds(pl.multiple_of(i * TILE, TILE), TILE), :], field)
            for t in range(PER):
                g = s * FACES + i * PER + t
                q = part[t * BLOCK : (t + 1) * BLOCK]
                Q[g] = q
                acc = acc + rows8(B[g] * q)
            return acc

        return lax.fori_loop(0, ORDER // TILE, tile, acc)

    acc1 = stiff(0, zero8)
    acc1 = stiff(1, acc1)
    acc1 = stiff(2, acc1)
    acc1 = stiff(3, acc1)
    coarse_c.wait()
    coarse_middle(0)

    def jump_of(own, mate):
        return (own.astype(F32) - mate.astype(F32)).astype(BF16)

    def square(jump):
        d = jump.astype(F32)
        return rows8(d * d)

    def pull(i):
        send_up(i).wait_recv()
        g = low(i // HALF, i % HALF)
        jump_l = jump_of(TR[g], MT[i])
        Q[g] = Q[g] + mul_t(M[g], jump_l)
        j = SLOTS - 1 - i
        send_down(j).wait_recv()
        g = INV[j]
        jump_u = jump_of(TR[g], AB[j])
        PP[j] = mul_t(M[g], jump_u)
        return jump_l, jump_u

    def pull_count(i, acc):
        jump_l, jump_u = pull(i)
        return acc + square(jump_l) + square(jump_u)

    acc1 = lax.fori_loop(0, UP, pull_count, acc1)

    def sum_start(p, values):
        for i, v in enumerate(values):
            AS[p, 0, i : i + 1, :] = one_row(v)
        AS[p, 0, len(values) : 8, :] = jnp.zeros((8 - len(values), COLS), F32)
        start_all(sum_grp, p, N_GRP)

    def sum_middle(p, row, extra):
        take_all(sum_grp, p, N_GRP)
        total = AS[p, 0]
        for d in range(1, N_GRP):
            total = total + AG[p, d - 1]
        AS[p, 1] = total
        AS[p, 1, row : row + 1, :] = AS[p, 1, row : row + 1, :] + extra
        start_all(sum_sub, p, N_SUB)

    def sum_end(p):
        take_all(sum_sub, p, N_SUB)
        total = AS[p, 1]
        for d in range(1, N_SUB):
            total = total + AZ[p, d - 1]
        return total

    sum_start(0, [acc0, acc1])
    coarse_val, coarse_energy = coarse_end(0, None)
    CA[...] = jnp.dot(OH[...], coarse_val, precision=EXACT, preferred_element_type=F32)

    @pl.loop(0, SUBDOMS)
    def _(s):
        for f in range(FACES):
            g = s * FACES + f
            Q[g, 0:1, :] = Q[g, 0:1, :] + CA[pl.ds(g, 1), :]

    @pl.loop(UP, 12)
    def _(i):
        pull(i)

    sum_middle(0, 1, coarse_energy)

    @pl.loop(12, SLOTS)
    def _(i):
        pull(i)

    def image_send(i, none):
        j = UP + i
        g = low(j // HALF, j % HALF)
        TQ[g] = mul(M[g], Q[g].astype(BF16)).astype(BF16)
        send_down2(j).start()
        g = INV[i]
        SU2[i] = mul(M[g], (Q[g] + PP[i]).astype(BF16)).astype(BF16)
        send_up2(i).start()
        return none

    lax.fori_loop(0, UP, image_send, 0)

    @pl.loop(0, SUBDOMS)
    def _(s):
        for f in range(FACES):
            g = s * FACES + f
            row = Q[g, 0:1, :]
            if f < HALF:
                row = row + PP[partner[s, f], 0:1, :]
            CR[pl.ds(g, 1), :] = row

    coarse_start(1)

    @pl.loop(0, UP)
    def _(i):
        g = low(i // HALF, i % HALF)
        TQ[g] = mul(M[g], Q[g].astype(BF16)).astype(BF16)
        g = INV[UP + i]
        TU[i] = mul(M[g], (Q[g] + PP[UP + i]).astype(BF16)).astype(BF16)

    sums = sum_end(0)
    norm0, curve0 = sums[0:1], sums[1:2]
    step0 = norm0 / curve0

    def resid(s, carry):
        n1, gq = carry
        for f in range(FACES):
            g = s * FACES + f
            q = Q[g]
            if f < HALF:
                q = q + PP[partner[s, f]]
            r = B[g] - step0 * q
            Q[g] = r
            RB[g] = r.astype(BF16)
            n1, gq = n1 + rows8(r * r), gq + rows8(r * q)
        return n1, gq

    acc_n, acc_g = lax.fori_loop(0, SUBDOMS, resid, (zero8, zero8))

    def inner(s, acc):
        for half in range(2):
            at = s * FACES + half * HALF
            own = RB[at : at + HALF].reshape(ORDER // 2, COLS)
            rows = pl.ds(half * (ORDER // 2), ORDER // 2)
            part = mul(S[s, rows, rows], own * jnp.asarray(0.5, BF16))
            if half == 0:
                other = RB[at + HALF : at + FACES].reshape(ORDER // 2, COLS)
                part = part + mul(S[s, rows, pl.ds(ORDER // 2, ORDER // 2)], other)
            for t in range(HALF):
                acc = acc + rows8(Q[at + t] * part[t * BLOCK : (t + 1) * BLOCK])
        return acc

    energy = inner(0, zero8)
    energy = inner(1, energy)
    coarse_middle(1)
    energy = inner(2, energy)
    energy = inner(3, energy)
    energy = energy + energy

    def pair2(first_jump, own, mate):
        d = first_jump.astype(F32) - step0 * (own.astype(F32) - mate.astype(F32))
        return rows8(d * d)

    def pair_low(j, acc):
        send_up2(j).wait_recv()
        g = low(j // HALF, j % HALF)
        return acc + pair2(jump_of(TR[g], MT[j]), TQ[g], RU2[j])

    def pair_up(j, acc):
        send_down2(j).wait_recv()
        g = INV[j]
        return acc + pair2(jump_of(TR[g], AB[j]), TU[j - UP], RD2[j - UP])

    energy = lax.fori_loop(UP, SLOTS, pair_up, energy)
    energy = lax.fori_loop(0, UP, pair_low, energy)

    sum_start(1, [acc_n, acc_g, energy])
    _, coarse_energy = coarse_end(1, step0)
    sum_middle(1, 2, coarse_energy)

    @pl.loop(0, SLOTS)
    def _(j):
        send_down(j).wait_send()
        send_up(j).wait_send()

    @pl.loop(0, UP)
    def _(j):
        send_up2(j).wait_send()

    @pl.loop(UP, SLOTS)
    def _(j):
        send_down2(j).wait_send()

    for p in range(2):
        end_all(scatter_rows, p, N_GRP)
        end_all(gather_rows, p, N_GRP)
        end_all(sum_grp, p, N_GRP)
    end_all(sum_sub, 0, N_SUB)

    sums = sum_end(1)
    norm1, cross, energy1 = sums[0:1], sums[1:2], sums[2:3]
    beta = norm1 / norm0
    curve1 = energy1 + 2.0 * beta * cross + beta * beta * curve0
    step1 = norm1 / curve1
    with_load = step0 + step1 * beta

    @pl.loop(0, SUBDOMS)
    def _(s):
        for f in range(FACES):
            g = s * FACES + f
            Q[g] = with_load * B[g] + step1 * Q[g]

    end_all(sum_sub, 1, N_SUB)


def on_device(schur, mortar, partner, corner_map, coarse_inv, load):
    vm, dma = pltpu.VMEM, pltpu.SemaphoreType.DMA
    anywhere = pl.BlockSpec(memory_space=pl.ANY)
    scalar = pl.BlockSpec(memory_space=pltpu.SMEM)
    faces_half = (ALL, BLOCK, COLS)
    slots_half = (SLOTS, BLOCK, COLS)
    scratch = [
        vm((SUBDOMS, ORDER, ORDER), BF16),
        vm((ALL, BLOCK, BLOCK), BF16),
        vm(faces_half, F32),
        vm((COARSE, COARSE), F32),
        vm(faces_half, BF16),
        vm(faces_half, BF16),
        vm(faces_half, BF16),
        vm(slots_half, BF16),
        vm(slots_half, BF16),
        vm(slots_half, BF16),
        vm(slots_half, F32),
        vm(faces_half, BF16),
        vm((SLOTS - UP, BLOCK, COLS), BF16),
        vm((UP, BLOCK, COLS), BF16),
        vm((UP, BLOCK, COLS), BF16),
        vm((SLOTS - UP, BLOCK, COLS), BF16),
        vm((ALL, COARSE), F32),
        vm((ALL, COLS), F32),
        vm((ALL, COLS), F32),
        vm((2, N_GRP, OWN, COLS), F32),
        vm((2, N_GRP - 1, OWN, COLS), F32),
        vm((2, N_GRP, OWN, COLS), F32),
        vm((2, 2, 8, COLS), F32),
        vm((2, N_GRP - 1, 8, COLS), F32),
        vm((2, N_SUB - 1, 8, COLS), F32),
        pltpu.SMEM((SLOTS,), jnp.int32),
        dma((SUBDOMS,)), dma, dma((SUBDOMS,)), dma,
        dma((SLOTS,)), dma((SLOTS,)), dma((SLOTS,)), dma((SLOTS,)),
        dma((SLOTS - UP,)), dma((SLOTS - UP,)), dma((UP,)), dma((UP,)),
        dma((2, 3, N_GRP - 1)), dma((2, 3, N_GRP - 1)),
        dma((2, N_SUB - 1)), dma((2, N_SUB - 1)),
    ]
    out = pl.pallas_call(
        kernel,
        out_shape=vm(faces_half, F32),
        in_specs=[anywhere] * 4 + [scalar] * 2,
        out_specs=pl.BlockSpec(memory_space=pltpu.VMEM),
        scratch_shapes=scratch,
        compiler_params=pltpu.CompilerParams(
            collective_id=0, has_side_effects=True, vmem_limit_bytes=52 * 1024 * 1024
        ),
    )(
        schur,
        mortar.reshape(ALL, BLOCK, BLOCK),
        load.reshape(ALL, BLOCK, COLS),
        coarse_inv,
        partner,
        corner_map,
    )
    return out.reshape(SUBDOMS, ORDER, COLS)


def solution(mesh):
    return jax.shard_map(
        on_device,
        mesh=mesh,
        in_specs=(
            P(("sub", "grp"), None, None),
            P(("sub", "grp"), None, None, None),
            P(("sub", "grp"), None),
            P(("sub", "grp"), None),
            P("sub", None, None),
            P(("sub", "grp"), None, None),
        ),
        out_specs=P(("sub", "grp"), None, None),
        check_vma=False,
    )
```
